32 devices in a mesh: groups: 2 (over x), wide: 16 (over z, y, core).
Axes of the slice: x: 2, y: 2, z: 4, core: 2. Of those that a mesh axis runs over, the one named last changes fastest.
Arguments:
- queries: bfloat16 [128, 16, 1024], P(('groups', 'wide')), parts along dimension 0, may hold values from -6.5 to 6.5
- cache_keys: bfloat16 [128, 1024, 128], P(('groups', 'wide')), parts along dimension 0, may hold values from -6.5 to 6.5
- cache_values: bfloat16 [128, 1024, 128], P(('groups', 'wide')), parts along dimension 0, may hold values from -32 to 32
- new_keys: bfloat16 [128, 16, 128], P(('groups', 'wide')), parts along dimension 0, may hold values from -15 to 15
- new_values: bfloat16 [128, 16, 128], P(('groups', 'wide')), parts along dimension 0, may hold values from -32 to 32
- cache_lengths: int32 [16], P('groups'), parts along dimension 0, may hold values from 64 to 1024, as said below
- step_segments: int32 [16, 16], P('groups'), parts along dimension 0, may hold values from 0 to 3, never falling along the last dimension, each value on 1 to 8 neighbouring positions
- resid_in: bfloat16 [256, 8192], P('groups', 'wide'), parts along dimension 0, may hold values from -70 to 70
- out_weight: bfloat16 [8192, 8192], P(None, 'wide'), may hold values from -0.0625 to 0.0625
- norm_gain: float32 [8192], replicated, may hold values from 0.1 to 1.9
- gate_weight: bfloat16 [8192, 16384], P(None, 'wide'), may hold values from -0.0625 to 0.0625
- up_weight: bfloat16 [8192, 16384], P(None, 'wide'), may hold values from -0.0625 to 0.0625
Outputs:
- residual: bfloat16 [256, 8192], P('groups', 'wide'), parts along dimension 0
- activ: bfloat16 [256, 16384], P('groups', 'wide'), parts along dimension 0
The draws below stay inside these ranges and needn't reach their ends.
There are 2 independent parts, one for each index of `groups`. The reference program is written for one: setup_inputs(seed, part) draws one part's arguments, and reference() takes and returns one part's arrays. A program takes and returns all parts, laid end to end along the dimension named above; an argument that names none is the same for every part. Nothing has to cross between parts.
Inputs may be any that keep to these rules, and one draw needn't show every extreme that they name: `cache_lengths`: some beam has all 1024 slots live. `step_segments`: never falling along a beam's steps.
All inputs are finite; a program needn't handle non-finite values.
Results may differ from the reference program's by a relative error of at most 0.0082.
Values may be sent and summed in bfloat16 or wider, within the bound.
No kernel may reach another device: no remote copies, remote signals or barrier semaphores. Data moves between devices by JAX's collectives and lax.ppermute only.
A program may use at most 128 MiB of HBM per device.

```python
import math
import jax
import jax.numpy as jnp
import numpy as np
from jax import lax

D = 8192
KVH = 8
HD = 128
FFW = 16384
STEPS = 16
CLEN = 1024
GQ = 8
BEAMS = 8
PAIRS = 64
TOKENS = 128


def draw_queries(key, part):
    base_key = jax.random.fold_in(key, 11)
    values = jnp.clip(jax.random.normal(base_key, (PAIRS, STEPS, GQ * HD), jnp.float32), -4.5, 4.5)
    return values.astype(jnp.bfloat16)


def draw_cache_keys(key, part):
    base_key = jax.random.fold_in(key, 13)
    values = jnp.clip(jax.random.normal(base_key, (PAIRS, CLEN, HD), jnp.float32), -4.5, 4.5)
    return values.astype(jnp.bfloat16)


def draw_cache_lengths(key, part):
    key_len, key_order = jax.random.split(jax.random.fold_in(key, 23))
    lengths = jax.random.randint(key_len, (BEAMS,), CLEN // 16, CLEN + 1)
    order = jax.random.permutation(key_order, BEAMS)
    lengths = lengths.at[order[0]].set(CLEN).at[order[1]].set(CLEN // 16)
    return lengths.astype(jnp.int32)


def draw_resid_in(key, part):
    key_rows, key_cols, key_base = jax.random.split(jax.random.fold_in(key, 31), 3)
    rise = jnp.exp(math.log(3.0) * jnp.arange(D, dtype=jnp.float32) / D)
    col_scale = rise * jnp.exp(jax.random.uniform(key_cols, (D,), jnp.float32, math.log(0.6), math.log(1.8)))
    row_scale = jnp.exp(jax.random.uniform(key_rows, (TOKENS,), jnp.float32, math.log(0.3), math.log(3.0)))
    base = jnp.clip(jax.random.normal(key_base, (TOKENS, D), jnp.float32), -4.0, 4.0)
    return (base * row_scale[:, None] * col_scale[None, :]).astype(jnp.bfloat16)


def block_levels(stream_key, extent, shards, smallest, high):
    def one(axis_at, shards_of):
        heights = jax.random.uniform(jax.random.fold_in(jax.random.fold_in(stream_key, 6), axis_at), (shards_of,), jnp.float32, smallest / len(shards), high / len(shards))
        return jnp.repeat(jnp.exp(heights), extent[axis_at] // shards_of).reshape((-1,) + (1,) * (len(extent) - axis_at - 1))

    loudness = one(*shards[0])
    for cut in shards[1:]:
        loudness = loudness * one(*cut)
    return loudness


def split_up(count, total, bound, skew):
    weights = [(1 << 20) // math.isqrt(grade ** skew) + 1 for grade in range(2, count + 1)]
    spare, given = total - bound - (count - 1), [1] * (count - 1)
    while spare > 0:
        movable = [i for i in range(count - 1) if given[i] < bound]
        pool, left = sum([weights[i] for i in movable]), spare
        for i in movable:
            more = min(bound - given[i], max(1, left * weights[i] // pool), spare)
            given[i] = given[i] + more
            spare = spare - more
    return np.array([bound] + given)


def ragged_sizes(rng, count, total, limit, lean):
    if count == 2:
        one = jax.random.randint(rng, (), max(1, total - limit), min(limit, total - 1) + 1)
        return jnp.stack([one, total - one])
    sizes = jnp.asarray(split_up(count, total, limit, lean), jnp.int32)
    couples = (count - 1) // 2
    giver, receiver = sizes[1:1 + 2 * couples:2], sizes[2:2 + 2 * couples:2]
    room = jnp.minimum(giver - 1, limit - receiver)
    passed = jax.random.randint(jax.random.fold_in(rng, 1), (couples,), 0, 1 << 20) % (room + 1)
    sizes = sizes.at[1:1 + 2 * couples:2].set(giver - passed).at[2:2 + 2 * couples:2].set(receiver + passed)
    return sizes[jax.random.permutation(jax.random.fold_in(rng, 2), count)]


def bell_draw(own_key, extent, scale, bound, shards=(), held_as=jnp.bfloat16):
    drawn = scale * jax.random.normal(own_key, extent, jnp.float32)
    if shards:
        drawn = drawn * block_levels(own_key, extent, shards, -0.22, 0.18)
    return jnp.clip(drawn, -bound, bound).astype(held_as)


def setup_inputs(seed: int = 0, part: int = 0) -> dict:
    splits = jax.random.split(jax.random.key(seed), 13)
    part_keys = jax.random.split(jax.random.fold_in(splits[12], part), 13)
    return {
        "queries": draw_queries(jax.random.fold_in(jax.random.fold_in(splits[12], part), 71), part),
        "cache_keys": draw_cache_keys(jax.random.fold_in(jax.random.fold_in(splits[12], part), 71), part),
        "cache_values": bell_draw(part_keys[2], (PAIRS, CLEN, HD), 8.0, 32.0, ((0, 16),)),
        "new_keys": bell_draw(part_keys[3], (PAIRS, STEPS, HD), 3.0, 15.0, ((0, 16),)),
        "new_values": bell_draw(part_keys[4], (PAIRS, STEPS, HD), 8.0, 32.0, ((0, 16),)),
        "cache_lengths": draw_cache_lengths(jax.random.fold_in(jax.random.fold_in(splits[12], part), 71), part),
        "step_segments": jax.vmap(lambda own: jnp.searchsorted(jnp.cumsum(ragged_sizes(own, STEPS // 4, STEPS, STEPS // 2, 1)), jnp.arange(STEPS), side="right"))(jax.random.split(part_keys[6], BEAMS)).reshape((BEAMS, STEPS)).astype(jnp.int32),
        "resid_in": draw_resid_in(jax.random.fold_in(jax.random.fold_in(splits[12], part), 71), part),
        "out_weight": bell_draw(splits[8], (D, D), D ** -0.5, 0.0625, ((1, 16),)),
        "norm_gain": jnp.clip(1.0 + 0.18 * jax.random.normal(splits[9], (D,), jnp.float32), 0.1, 1.9),
        "gate_weight": bell_draw(splits[10], (D, FFW), D ** -0.5, 0.0625, ((1, 16),)),
        "up_weight": bell_draw(splits[11], (D, FFW), D ** -0.5, 0.0625, ((1, 16),)),
    }


def reference(queries, cache_keys, cache_values, new_keys, new_values, cache_lengths, step_segments, resid_in, out_weight, norm_gain, gate_weight, up_weight):
    beam_of = jnp.arange(PAIRS, dtype=jnp.int32) % BEAMS
    live_length = cache_lengths[beam_of]
    segment_ids = step_segments[beam_of]
    query_heads = queries.astype(jnp.float32).reshape(PAIRS, STEPS, GQ, HD)
    all_keys = jnp.concatenate([cache_keys, new_keys], axis=1).astype(jnp.float32)
    all_values = jnp.concatenate([cache_values, new_values], axis=1).astype(jnp.float32)
    score_scale = 1.0 / math.sqrt(HD)
    scores = jnp.einsum('psgd,pkd->psgk', query_heads, all_keys) * score_scale
    slot_pos = jnp.arange(CLEN, dtype=jnp.int32)
    old_live = slot_pos[None, :] < live_length[:, None]
    step_pos = jnp.arange(STEPS, dtype=jnp.int32)
    same_segment = segment_ids[:, None, :] == segment_ids[:, :, None]
    new_live = same_segment & (step_pos[None, None, :] <= step_pos[None, :, None])
    live = jnp.concatenate([jnp.broadcast_to(old_live[:, None, :], (PAIRS, STEPS, CLEN)), new_live], axis=2)
    scores = jnp.where(live[:, :, None, :], scores, -jnp.inf)
    row_max = lax.optimization_barrier(jnp.max(scores, axis=3, keepdims=True))
    expon = jnp.exp(scores - row_max)
    weights = (expon / lax.optimization_barrier(jnp.sum(expon, axis=3, keepdims=True))).astype(jnp.bfloat16)
    mixed = jnp.einsum('psgk,pkd->psgd', weights.astype(jnp.float32), all_values)
    attention = mixed.astype(jnp.bfloat16).reshape(KVH, TOKENS, GQ * HD)
    attention = jnp.transpose(attention, (1, 0, 2)).reshape(TOKENS, D)
    projected = jnp.dot(attention, out_weight, preferred_element_type=jnp.float32)
    residual = (resid_in.astype(jnp.float32) + projected).astype(jnp.bfloat16)
    wide_rows = residual.astype(jnp.float32)
    inverse = lax.rsqrt(lax.optimization_barrier(jnp.sum(wide_rows * wide_rows, axis=1)) / D + 1e-06)
    normed = (wide_rows * inverse[:, None] * norm_gain[None, :]).astype(jnp.bfloat16)
    gate = jnp.dot(normed, gate_weight, preferred_element_type=jnp.float32)
    up_part = jnp.dot(normed, up_weight, preferred_element_type=jnp.float32)
    activ = (jax.nn.silu(gate) * up_part).astype(jnp.bfloat16)
    return (residual, activ)
```

```python
import math

import jax
import jax.numpy as jnp
from jax import lax
from jax.experimental import pallas as pl
from jax.experimental.pallas import tpu as pltpu
from jax.sharding import PartitionSpec as P

VMEM = pl.BlockSpec(memory_space=pltpu.VMEM)


def layout(size):
    cores = 2 if size % 2 == 0 else 1
    rows = 2 if (size // cores) % 2 == 0 else 1
    return size // (cores * rows), rows, cores


def attend(first_pair, queries, cache_keys, cache_values, new_keys, new_values, lengths, segments):
    pairs, steps, width = queries.shape
    slots, head = cache_keys.shape[1:]
    heads = width // head
    beams = lengths.shape[0]
    scale = 1.0 / math.sqrt(head)

    def kernel(first, lens, segs, q_ref, k_ref, v_ref, nk_ref, nv_ref, o_ref):
        beam = lax.rem(first[0] + pl.program_id(0), beams)
        q = q_ref[0]
        q = jnp.concatenate([q[:, i * head : (i + 1) * head] for i in range(heads)], axis=0)
        contract = (((1,), (1,)), ((), ()))
        old = lax.dot_general(q, k_ref[0], contract, preferred_element_type=jnp.float32) * scale
        new = lax.dot_general(q, nk_ref[0], contract, preferred_element_type=jnp.float32) * scale
        slot = lax.broadcasted_iota(jnp.int32, old.shape, 1)
        old = jnp.where(slot < lens[beam], old, -jnp.inf)
        row = lax.broadcasted_iota(jnp.int32, (steps, steps), 0)
        col = lax.broadcasted_iota(jnp.int32, (steps, steps), 1)
        seg_row = jnp.zeros((steps, steps), jnp.int32)
        seg_col = jnp.zeros((steps, steps), jnp.int32)
        for j in range(steps):
            value = segs[beam, j]
            seg_row = jnp.where(row == j, value, seg_row)
            seg_col = jnp.where(col == j, value, seg_col)
        bias = jnp.where((seg_row == seg_col) & (col <= row), 0.0, -jnp.inf)
        new = new + jnp.concatenate([bias] * heads, axis=0)
        top = jnp.maximum(
            jnp.max(old, axis=1, keepdims=True), jnp.max(new, axis=1, keepdims=True)
        )
        old = jnp.exp(old - top)
        new = jnp.exp(new - top)
        denom = jnp.sum(old, axis=1, keepdims=True) + jnp.sum(new, axis=1, keepdims=True)
        inverse = 1.0 / denom
        mixed = jnp.dot(
            (old * inverse).astype(jnp.bfloat16), v_ref[0], preferred_element_type=jnp.float32
        ) + jnp.dot(
            (new * inverse).astype(jnp.bfloat16), nv_ref[0], preferred_element_type=jnp.float32
        )
        mixed = mixed.astype(jnp.bfloat16)
        for i in range(heads):
            o_ref[:, i * head : (i + 1) * head] = mixed[i * steps : (i + 1) * steps]

    def whole(*shape):
        return pl.BlockSpec((1, *shape), lambda p, *_: (p, 0, 0))

    return pl.pallas_call(
        kernel,
        grid_spec=pltpu.PrefetchScalarGridSpec(
            num_scalar_prefetch=3,
            grid=(pairs,),
            in_specs=[
                whole(steps, width),
                whole(slots, head),
                whole(slots, head),
                whole(steps, head),
                whole(steps, head),
            ],
            out_specs=pl.BlockSpec((steps, width), lambda p, *_: (p, 0)),
        ),
        out_shape=jax.ShapeDtypeStruct((pairs * steps, width), jnp.bfloat16),
        compiler_params=pltpu.CompilerParams(vmem_limit_bytes=16 << 20),
        cost_estimate=pl.CostEstimate(
            flops=4 * pairs * steps * heads * slots * head,
            bytes_accessed=4 * pairs * slots * head,
            transcendentals=pairs * steps * heads * slots,
        ),
        name="attend",
    )(first_pair, lengths, segments, queries, cache_keys, cache_values, new_keys, new_values)


def spread(x, size):
    planes, rows, cores = layout(size)
    line = rows * cores
    assert cores == 2 and rows == 2

    def send(value, target):
        return lax.ppermute(value, "wide", [(i, target(i)) for i in range(size)])

    def shift(value, k):
        return send(value, lambda i: (i + k * line) % size)

    def cross(value):
        return send(value, lambda i: i ^ cores)

    def both(value):
        return value, send(value, lambda i: i ^ 1)

    def after(value, *others):
        return lax.optimization_barrier((value, *others))[0]

    rounds = [[both(x)]]
    near = sorted({1, planes - 1}) if planes > 1 else []
    far = [k for k in range(2, planes - 1)]
    got = [(k, shift(x, k)) for k in near]
    rounds.append([both(cross(x))])
    start = after(x, *[v for _, v in got])
    later = [(k, shift(start, k)) for k in far]
    for group in (got, later):
        if group:
            rounds.append([both(v) for _, v in group])
            rounds.append([both(cross(v)) for _, v in group])
    order = [(0, 0), (0, 1)]
    for group in (near, far):
        order += [(k, 0) for k in group] + [(k, 1) for k in group]
    return rounds, order


def project(table, base, first, last, acc, blocks, resid, weight, width, tokens):
    cols = weight.shape[1]
    half = blocks[0][0].shape[0]
    count = len(blocks)

    def kernel(tab, *refs):
        refs = list(refs)
        xs = [(refs.pop(0), refs.pop(0)) for _ in range(count)]
        w_ref = refs.pop(0)
        acc_ref = None if first else refs.pop(0)
        resid_ref = refs.pop(0) if last else None
        o_ref, joined, *rest = refs
        total = rest[0] if last else o_ref
        step = pl.program_id(0)

        @pl.when(step == 0)
        def _():
            total[...] = jnp.zeros_like(total) if first else acc_ref[...]

        own = tab[0, 0]
        for i in range(count):

            @pl.when(step == i)
            def _(i=i):
                joined[pl.ds(pl.multiple_of(own * half, half), half)] = xs[i][0][...]
                joined[pl.ds(pl.multiple_of((1 - own) * half, half), half)] = xs[i][1][...]

        at = pl.ds(pl.multiple_of(tab[2, base + step] * (2 * half), 2 * half), 2 * half)
        total[at] += jnp.dot(joined[...], w_ref[...], preferred_element_type=jnp.float32)
        if last:

            @pl.when(step == count - 1)
            def _():
                o_ref[...] = (resid_ref[...].astype(jnp.float32) + total[...]).astype(
                    jnp.bfloat16
                )

    inputs = [v for pair in blocks for v in pair] + [weight]
    specs = [pl.BlockSpec((half, width), lambda j, t: (0, 0))] * (2 * count) + [
        pl.BlockSpec((width, cols), lambda j, t: (t[1, base + j], 0))
    ]
    full = pl.BlockSpec((tokens, cols), lambda j, t: (0, 0))
    if not first:
        inputs.append(acc)
        specs.append(full)
    if last:
        inputs.append(resid)
        specs.append(full)
    scratch = [pltpu.VMEM((2 * half, width), jnp.bfloat16)]
    if last:
        scratch.append(pltpu.VMEM((tokens, cols), jnp.float32))
    return pl.pallas_call(
        kernel,
        grid_spec=pltpu.PrefetchScalarGridSpec(
            num_scalar_prefetch=1,
            grid=(count,),
            in_specs=specs,
            out_specs=full,
            scratch_shapes=scratch,
        ),
        out_shape=jax.ShapeDtypeStruct((tokens, cols), jnp.bfloat16 if last else jnp.float32),
        compiler_params=pltpu.CompilerParams(vmem_limit_bytes=16 << 20),
        cost_estimate=pl.CostEstimate(
            flops=4 * count * half * width * cols,
            bytes_accessed=2 * count * width * cols,
            transcendentals=0,
        ),
        name="project",
    )(table, *inputs)


def expand(table, base, first, last, state, blocks, gain, gate_weight, up_weight):
    flat = [v for pair in blocks for v in pair]
    count = len(flat)
    tokens, depth = flat[0].shape
    cols = gate_weight.shape[1]
    features = gate_weight.shape[0]
    lanes = 128

    def kernel(tab, *refs):
        refs = list(refs)
        xs = [refs.pop(0) for _ in range(count)]
        gain_ref, g_ref, u_ref = refs.pop(0), refs.pop(0), refs.pop(0)
        olds = [] if first else [refs.pop(0) for _ in range(3)]
        o_ref = refs.pop(0) if last else None
        gate, up, square = refs
        step = pl.program_id(0)

        @pl.when(step == 0)
        def _():
            for i, total in enumerate((gate, up, square)):
                total[...] = jnp.zeros_like(total) if first else olds[i][...]

        def add(x_ref):
            wide = x_ref[...].astype(jnp.float32)
            squares = wide * wide
            part = squares[:, :lanes]
            for i in range(1, depth // lanes):
                part = part + squares[:, i * lanes : (i + 1) * lanes]
            square[...] += part
            scaled = (wide * gain_ref[0]).astype(jnp.bfloat16)
            gate[...] += jnp.dot(scaled, g_ref[...], preferred_element_type=jnp.float32)
            up[...] += jnp.dot(scaled, u_ref[...], preferred_element_type=jnp.float32)

        for i in range(count):
            pl.when(step == i)(lambda i=i: add(xs[i]))
        if last:

            @pl.when(step == count - 1)
            def _():
                mean = jnp.sum(square[...], axis=1, keepdims=True) / features
                inverse = lax.rsqrt(mean + 1e-06)
                v = gate[...] * inverse
                o_ref[...] = (v / (1.0 + jnp.exp(-v)) * (up[...] * inverse)).astype(jnp.bfloat16)

    def row(j, t):
        return (t[3, base + j], 0)

    sums = [(tokens, cols), (tokens, cols), (tokens, lanes)]
    specs = [pl.BlockSpec((tokens, depth), lambda j, t: (0, 0))] * count + [
        pl.BlockSpec((1, 1, depth), lambda j, t: (t[3, base + j], 0, 0)),
        pl.BlockSpec((depth, cols), row),
        pl.BlockSpec((depth, cols), row),
    ]
    sum_specs = [pl.BlockSpec(s, lambda j, t: (0, 0)) for s in sums]
    sum_shapes = [jax.ShapeDtypeStruct(s, jnp.float32) for s in sums]
    if not first:
        specs += sum_specs
    return pl.pallas_call(
        kernel,
        grid_spec=pltpu.PrefetchScalarGridSpec(
            num_scalar_prefetch=1,
            grid=(count,),
            in_specs=specs,
            out_specs=sum_specs[0] if last else sum_specs,
            scratch_shapes=[pltpu.VMEM(s, jnp.float32) for s in sums] if last else [],
        ),
        out_shape=jax.ShapeDtypeStruct((tokens, cols), jnp.bfloat16) if last else sum_shapes,
        compiler_params=pltpu.CompilerParams(vmem_limit_bytes=24 << 20),
        cost_estimate=pl.CostEstimate(
            flops=4 * count * tokens * depth * cols,
            bytes_accessed=4 * count * depth * cols,
            transcendentals=0,
        ),
        name="expand",
    )(table, *flat, gain, gate_weight, up_weight, *([] if first else state))


def make(size):
    planes, rows, cores = layout(size)

    def per_device(
        queries,
        cache_keys,
        cache_values,
        new_keys,
        new_values,
        cache_lengths,
        step_segments,
        resid_in,
        out_weight,
        norm_gain,
        gate_weight,
        up_weight,
    ):
        pairs, steps, width = queries.shape
        beams = cache_lengths.shape[0]
        tokens, depth = resid_in.shape
        assert beams % (cores * pairs) == 0
        me = lax.axis_index("wide")
        attention = attend(
            jnp.full((1,), me * pairs, jnp.int32),
            queries,
            cache_keys,
            cache_values,
            new_keys,
            new_values,
            cache_lengths,
            step_segments,
        )
        rounds, order = spread(attention, size)
        plane, row, core = me // (rows * cores), me // cores % rows, me % cores
        shifts = jnp.array([k for k, _ in order], jnp.int32)
        flips = jnp.array([f for _, f in order], jnp.int32)
        chip = (plane - shifts + planes) % planes * rows + row * (1 - flips) + (1 - row) * flips
        pair_at = chip * (cores * pairs)
        head_at = pair_at // beams
        token_at = pair_at % beams // (cores * pairs)
        chips = len(order)
        devices = chip[:, None] * cores + jnp.array([0, 1], jnp.int32)[None, :] * (1 - 2 * core) + core
        table = jnp.zeros((4, chips * cores), jnp.int32)
        table = table.at[0, 0].set(core).at[1, :chips].set(head_at).at[2, :chips].set(token_at)
        table = table.at[3].set(devices.reshape(-1))
        acc, base = None, 0
        for i, blocks in enumerate(rounds):
            acc = project(
                table,
                base,
                i == 0,
                i == len(rounds) - 1,
                acc,
                blocks,
                resid_in,
                out_weight,
                width,
                tokens,
            )
            base += len(blocks)
        residual = acc
        rounds, _ = spread(residual, size)
        gain = norm_gain.reshape(size, 1, depth)
        state, base = None, 0
        for i, blocks in enumerate(rounds):
            state = expand(
                table,
                base,
                i == 0,
                i == len(rounds) - 1,
                state,
                blocks,
                gain,
                gate_weight,
                up_weight,
            )
            base += cores * len(blocks)
        return residual, state

    return per_device


def solution(mesh):
    placed = (
        P(("groups", "wide"), None, None),
        P(("groups", "wide"), None, None),
        P(("groups", "wide"), None, None),
        P(("groups", "wide"), None, None),
        P(("groups", "wide"), None, None),
        P("groups"),
        P("groups", None),
        P("groups", "wide"),
        P(None, "wide"),
        P(),
        P(None, "wide"),
        P(None, "wide"),
    )
    return jax.shard_map(
        make(mesh.shape["wide"]),
        mesh=mesh,
        in_specs=placed,
        out_specs=(P("groups", "wide"), P("groups", "wide")),
        check_vma=False,
    )
```
